32 devices in a mesh: shard: 4 (over y, x), replica: 8 (over z, core).
Axes of the slice: x: 2, y: 2, z: 4, core: 2. Of those that a mesh axis runs over, the one named last changes fastest.
Arguments:
- hidden_in: bfloat16 [32, 212, 960], P(('shard', 'replica')), may hold values from -9 to 9
- cotangent: bfloat16 [32, 212, 960], P(('shard', 'replica')), may hold values from -6 to 6
- segment_ids: int32 [32, 212], P(('shard', 'replica')), may hold values from 0 to 6, as said below
- positions: int32 [32, 212], P(('shard', 'replica')), may hold values from 0 to 211, as said below
- w_qkv: bfloat16 [960, 1600], P(None, 'shard'), may hold values from -1 to 1
- w_out: bfloat16 [960, 960], P(None, 'shard'), may hold values from -0.5 to 0.5
- w_gate: bfloat16 [960, 2560], P(None, 'shard'), may hold values from -0.1875 to 0.1875
- w_up: bfloat16 [960, 2560], P(None, 'shard'), may hold values from -0.1875 to 0.1875
- w_down: bfloat16 [2560, 960], P('shard'), may hold values from -0.25 to 0.25
- gain_attn: bfloat16 [960], P('shard'), may hold values from 0.5 to 1.5
- gain_mlp: bfloat16 [960], P('shard'), may hold values from 0.5 to 1.5
Outputs:
- hidden_out: bfloat16 [32, 212, 960], P(('shard', 'replica'))
- grad_input: float32 [32, 212, 960], P(('shard', 'replica'))
- grad_qkv: float32 [960, 1600], P(None, 'shard')
- grad_out: float32 [960, 960], P(None, 'shard')
- grad_gate: float32 [960, 2560], P(None, 'shard')
- grad_up: float32 [960, 2560], P(None, 'shard')
- grad_down: float32 [2560, 960], P('shard')
- grad_gain_attn: float32 [960], P('shard')
- grad_gain_mlp: float32 [960], P('shard')
The draws below stay inside these ranges and needn't reach their ends.
Inputs may be any that keep to these rules, and one draw needn't show every extreme that they name: `segment_ids`: within each sequence the numbers start at 0 and never fall; a run of equal numbers is one document. `positions`: the offset of each token from the first token of its document.
All inputs are finite; a program needn't handle non-finite values.
Results may differ from the reference program's by a relative error of at most 0.022.
Values may be sent and summed in bfloat16 or wider, within the bound.
A program may use at most 128 MiB of HBM per device.

```python
import math
import jax
import jax.numpy as jnp
from jax import lax

D = 960
H = 15
KV = 5
HD = 64
FF = 2560
LEN = 212
SEQ_DEV = 1
QKV = 1600
SEQS = 32
N_SHARD = 4


def documents(key):
    base_key = jax.random.fold_in(key, 11)
    cut_key, keep_key = jax.random.split(base_key)
    stride = (LEN - 1) // 6
    offsets = jax.random.randint(cut_key, (SEQS, 6), 0, stride)
    cut_points = 1 + jnp.arange(6, dtype=jnp.int32)[None, :] * stride + offsets
    keep_flags = jax.random.randint(keep_key, (SEQS, 6), 0, 2)
    row_id = jnp.arange(SEQS, dtype=jnp.int32)[:, None]
    keep_flags = jnp.where(row_id == 0, 0, jnp.where(row_id == 1, 1, keep_flags))
    column = jnp.arange(LEN, dtype=jnp.int32)
    cut_hits = (cut_points[:, :, None] == column[None, None, :]) & (keep_flags[:, :, None] == 1)
    starts = jnp.any(cut_hits, axis=1)
    segment = jnp.cumsum(starts.astype(jnp.int32), axis=1)
    begins = lax.cummax(jnp.where(starts, column[None, :], 0), axis=1)
    return (segment.astype(jnp.int32), (column[None, :] - begins).astype(jnp.int32))


def draw_segment_ids(key, part):
    return documents(key)[0]


def draw_positions(key, part):
    return documents(key)[1]


def draw_hidden_in(key, part):
    shape = (SEQS, LEN, D)
    return jax.random.truncated_normal(jax.random.fold_in(key, 202), -6.0, 6.0, shape, jnp.float32).astype(jnp.bfloat16)


def draw_w_qkv(key, part):
    shape = (D, QKV)
    return (jax.random.truncated_normal(jax.random.fold_in(key, 302), -6.0, 6.0, shape, jnp.float32) * D ** (-0.5)).astype(jnp.bfloat16)


def level_of(stream_key, shape, cuts, least, largest):
    level, own = 1.0, jax.random.fold_in(stream_key, 6)
    for axis_at, shards_of in cuts:
        draws = jnp.exp(jax.random.uniform(jax.random.fold_in(own, axis_at), (shards_of,), jnp.float32, least / len(cuts), largest / len(cuts)))
        level = level * jnp.repeat(draws, shape[axis_at] // shards_of).reshape([-1 if axis == axis_at else 1 for axis in range(len(shape))])
    return level


def gaussian(rng, shape, deviation, limit, cuts=(), kind=jnp.bfloat16):
    level = level_of(rng, shape, cuts, -0.22, 0.18) if cuts else 1.0
    result = jax.random.normal(rng, shape, jnp.float32) * deviation * level
    return jnp.minimum(jnp.maximum(result, -limit), limit).astype(kind)


def setup_inputs(seed: int = 0) -> dict:
    arg_keys = jax.random.split(jax.random.key(seed), 12)
    hidden_in = draw_hidden_in(jax.random.fold_in(arg_keys[11], 71), 0)
    cotangent = gaussian(arg_keys[1], (SEQS, LEN, D), 1.0, 6.0, ((0, 32),))
    segment_ids = draw_segment_ids(jax.random.fold_in(arg_keys[11], 71), 0)
    positions = draw_positions(jax.random.fold_in(arg_keys[11], 71), 0)
    w_qkv = draw_w_qkv(jax.random.fold_in(arg_keys[11], 71), 0)
    w_out = gaussian(arg_keys[5], (H * HD, D), (H * HD // 8) ** -0.5, 0.5, ((1, 4),))
    w_gate = gaussian(arg_keys[6], (D, FF), D ** -0.5, 0.1875, ((1, 4),))
    w_up = gaussian(arg_keys[7], (D, FF), D ** -0.5, 0.1875, ((1, 4),))
    w_down = gaussian(arg_keys[8], (FF, D), (FF // 4) ** -0.5, 0.25, ((0, 4),))
    gain_attn = jnp.clip(1.0 + 0.1 * jax.random.normal(arg_keys[9], (D,), jnp.float32), 0.5, 1.5).astype(jnp.bfloat16)
    gain_mlp = jnp.clip(1.0 + 0.1 * jax.random.normal(arg_keys[10], (D,), jnp.float32), 0.5, 1.5).astype(jnp.bfloat16)
    return {"hidden_in": hidden_in, "cotangent": cotangent, "segment_ids": segment_ids, "positions": positions, "w_qkv": w_qkv, "w_out": w_out, "w_gate": w_gate, "w_up": w_up, "w_down": w_down, "gain_attn": gain_attn, "gain_mlp": gain_mlp}


EPSILON = 1e-05
THETA_BASE = 100000.0
NEG_FILL = -1e+30

def rope_tables(position_ids):
    half_width = HD // 2
    freq_steps = jnp.arange(half_width, dtype=jnp.float32) * (2.0 / HD)
    inverse = jnp.exp(-math.log(THETA_BASE) * freq_steps)
    angles = position_ids.astype(jnp.float32)[:, None] * inverse[None, :]
    cosine = jnp.cos(angles)
    sine_part = jnp.sin(angles)
    return (jnp.concatenate([cosine, cosine], -1), jnp.concatenate([sine_part, sine_part], -1))

def rotate(tensor, cosine, sine_part):
    half_width = HD // 2
    turned = jnp.concatenate([-tensor[..., half_width:], tensor[..., :half_width]], -1)
    return tensor * cosine[:, None, :] + turned * sine_part[:, None, :]

def rotate_back(gradient, cosine, sine_part):
    half_width = HD // 2
    scaled = gradient * sine_part[:, None, :]
    return gradient * cosine[:, None, :] + jnp.concatenate([scaled[..., half_width:], -scaled[..., :half_width]], -1)

def rounded(values):
    return lax.optimization_barrier(values.astype(jnp.bfloat16)).astype(jnp.float32)

def norm_forward(values, gain_row):
    inv_rms = lax.rsqrt(lax.optimization_barrier(jnp.mean(values * values, -1, keepdims=True)) + EPSILON)
    return ((values * inv_rms * gain_row.astype(jnp.float32)).astype(jnp.bfloat16), inv_rms)

def norm_backward(values, inv_rms, gain_row, grad_normed):
    weighted = grad_normed * gain_row.astype(jnp.float32)
    gain_grad = lax.optimization_barrier(jnp.sum(grad_normed * values * inv_rms, 0))
    inner_mean = lax.optimization_barrier(jnp.mean(weighted * values, -1, keepdims=True))
    return (inv_rms * weighted - values * inv_rms ** 3 * inner_mean, gain_grad)

def attention_forward(queries, keys_in, values_in, allowed):
    length = queries.shape[0]
    groups = H // KV
    scale_factor = HD ** (-0.5)
    query_g = queries.astype(jnp.float32).reshape(length, KV, groups, HD)
    scores = jnp.einsum('qkgd,skd->kgqs', query_g, keys_in.astype(jnp.float32)) * scale_factor
    scores = jnp.where(allowed, scores, NEG_FILL)
    highest = lax.optimization_barrier(jnp.max(scores, -1, keepdims=True))
    raw_weights = jnp.exp(scores - highest)
    totals = lax.optimization_barrier(jnp.sum(raw_weights, -1, keepdims=True))
    log_total = highest + jnp.log(totals)
    attn_probs = rounded(raw_weights / totals)
    mixed_vals = jnp.einsum('kgqs,skd->qkgd', attn_probs, values_in.astype(jnp.float32))
    return (mixed_vals.reshape(length, H * HD).astype(jnp.bfloat16), log_total)

def attention_backward(queries, keys_in, values_in, allowed, log_total, attended, grad_attended):
    length = queries.shape[0]
    groups = H // KV
    scale_factor = HD ** (-0.5)
    query_g = queries.astype(jnp.float32).reshape(length, KV, groups, HD)
    keys_f = keys_in.astype(jnp.float32)
    values_f = values_in.astype(jnp.float32)
    scores = jnp.einsum('qkgd,skd->kgqs', query_g, keys_f) * scale_factor
    scores = jnp.where(allowed, scores, NEG_FILL)
    attn_probs = jnp.exp(scores - log_total)
    probs_b = rounded(attn_probs)
    grad_g = grad_attended.astype(jnp.float32).reshape(length, KV, groups, HD)
    attended_g = attended.astype(jnp.float32).reshape(length, KV, groups, HD)
    grad_values = jnp.einsum('kgqs,qkgd->skd', probs_b, grad_g)
    grad_probs = jnp.einsum('qkgd,skd->kgqs', grad_g, values_f)
    delta_row = jnp.transpose(lax.optimization_barrier(jnp.sum(grad_g * attended_g, -1)), (1, 2, 0))[..., None]
    grad_scores = rounded(attn_probs * (grad_probs - delta_row) * scale_factor)
    grad_queries = jnp.einsum('kgqs,skd->qkgd', grad_scores, keys_f).reshape(length, H, HD)
    grad_keys = jnp.einsum('kgqs,qkgd->skd', grad_scores, query_g)
    return (grad_queries, grad_keys, grad_values)

def layer_block(rows_in, cot_in, segment_block, position_block, weights):
    w_qkv, w_out, w_gate, w_up, w_down, gain_attn, gain_mlp = weights
    per_group = rows_in.shape[0]
    row_total = per_group * LEN
    flat_rows = rows_in.reshape(row_total, D).astype(jnp.float32)
    cosine, sine_part = rope_tables(position_block.reshape(row_total))
    column = jnp.arange(LEN)
    causal = column[None, :] <= column[:, None]
    allowed = (segment_block[:, :, None] == segment_block[:, None, :]) & causal[None]
    normed_one, inv_one = norm_forward(flat_rows, gain_attn)
    projected = jnp.dot(normed_one, w_qkv, preferred_element_type=jnp.float32)
    queries = rotate(projected[:, :H * HD].reshape(row_total, H, HD), cosine, sine_part).astype(jnp.bfloat16)
    keys_b = rotate(projected[:, H * HD:(H + KV) * HD].reshape(row_total, KV, HD), cosine, sine_part).astype(jnp.bfloat16)
    values_b = projected[:, (H + KV) * HD:].reshape(row_total, KV, HD).astype(jnp.bfloat16)
    queries_s = queries.reshape(per_group, LEN, H, HD)
    keys_s = keys_b.reshape(per_group, LEN, KV, HD)
    values_s = values_b.reshape(per_group, LEN, KV, HD)
    attended_s, log_total = jax.vmap(attention_forward)(queries_s, keys_s, values_s, allowed)
    attended = attended_s.reshape(row_total, H * HD)
    middle = flat_rows + jnp.dot(attended, w_out, preferred_element_type=jnp.float32)
    normed_two, inv_two = norm_forward(middle, gain_mlp)
    gate_pre = jnp.dot(normed_two, w_gate, preferred_element_type=jnp.float32)
    up_pre = jnp.dot(normed_two, w_up, preferred_element_type=jnp.float32)
    sigmoid_val = jax.nn.sigmoid(gate_pre)
    silu_val = gate_pre * sigmoid_val
    silu_slope = sigmoid_val * (1.0 + gate_pre * (1.0 - sigmoid_val))
    activated = (silu_val * up_pre).astype(jnp.bfloat16)
    output_rows = middle + jnp.dot(activated, w_down, preferred_element_type=jnp.float32)
    hidden_out = output_rows.astype(jnp.bfloat16).reshape(rows_in.shape)
    cot_rows = cot_in.reshape(row_total, D)
    cot_float = cot_rows.astype(jnp.float32)
    grad_act = jnp.dot(cot_rows, w_down.T, preferred_element_type=jnp.float32)
    grad_up_b = (grad_act * silu_val).astype(jnp.bfloat16)
    grad_gate_b = (grad_act * up_pre * silu_slope).astype(jnp.bfloat16)
    grad_down = jnp.dot(activated.T, cot_rows, preferred_element_type=jnp.float32)
    grad_gate = jnp.dot(normed_two.T, grad_gate_b, preferred_element_type=jnp.float32)
    grad_up = jnp.dot(normed_two.T, grad_up_b, preferred_element_type=jnp.float32)
    grad_normed = jnp.dot(grad_gate_b, w_gate.T, preferred_element_type=jnp.float32) + jnp.dot(grad_up_b, w_up.T, preferred_element_type=jnp.float32)
    back_two, gain_two_grad = norm_backward(middle, inv_two, gain_mlp, grad_normed)
    grad_middle = cot_float + back_two
    grad_middle_b = grad_middle.astype(jnp.bfloat16)
    grad_out = jnp.dot(attended.T, grad_middle_b, preferred_element_type=jnp.float32)
    grad_attended = jnp.dot(grad_middle_b, w_out.T, preferred_element_type=jnp.float32).astype(jnp.bfloat16)
    grad_queries, grad_keys, grad_values = jax.vmap(attention_backward)(queries_s, keys_s, values_s, allowed, log_total, attended_s, grad_attended.reshape(per_group, LEN, H * HD))
    grad_queries = rotate_back(grad_queries.reshape(row_total, H, HD), cosine, sine_part)
    grad_keys = rotate_back(grad_keys.reshape(row_total, KV, HD), cosine, sine_part)
    grad_proj = jnp.concatenate([grad_queries.reshape(row_total, H * HD), grad_keys.reshape(row_total, KV * HD), grad_values.reshape(row_total, KV * HD)], 1).astype(jnp.bfloat16)
    grad_qkv = jnp.dot(normed_one.T, grad_proj, preferred_element_type=jnp.float32)
    grad_normed_one = jnp.dot(grad_proj, w_qkv.T, preferred_element_type=jnp.float32)
    back_one, gain_one_grad = norm_backward(flat_rows, inv_one, gain_attn, grad_normed_one)
    grad_input = (grad_middle + back_one).reshape(rows_in.shape)
    return (hidden_out, grad_input, (grad_qkv, grad_out, grad_gate, grad_up, grad_down, gain_one_grad, gain_two_grad))

def reference(hidden_in, cotangent, segment_ids, positions, w_qkv, w_out, w_gate, w_up, w_down, gain_attn, gain_mlp):
    per_block = SEQ_DEV * N_SHARD
    blocks = SEQS // per_block
    weights = (w_qkv, w_out, w_gate, w_up, w_down, gain_attn, gain_mlp)

    def advance(running, pieces):
        out_rows, grad_rows, fresh_grads = layer_block(pieces[0], pieces[1], pieces[2], pieces[3], weights)
        return (tuple((older + fresh_grad for older, fresh_grad in zip(running, fresh_grads))), (out_rows, grad_rows))
    initial = (jnp.zeros((D, QKV), jnp.float32), jnp.zeros((H * HD, D), jnp.float32), jnp.zeros((D, FF), jnp.float32), jnp.zeros((D, FF), jnp.float32), jnp.zeros((FF, D), jnp.float32), jnp.zeros((D,), jnp.float32), jnp.zeros((D,), jnp.float32))
    stacked = (hidden_in.reshape(blocks, per_block, LEN, D), cotangent.reshape(blocks, per_block, LEN, D), segment_ids.reshape(blocks, per_block, LEN), positions.reshape(blocks, per_block, LEN))
    totals, (outputs, grads_in) = lax.scan(advance, initial, stacked)
    return (outputs.reshape(SEQS, LEN, D), grads_in.reshape(SEQS, LEN, D), totals[0], totals[1], totals[2], totals[3], totals[4], totals[5], totals[6])
```

```python
import math

import jax
import jax.numpy as jnp
from jax import lax
from jax.sharding import PartitionSpec as P

D = 960
H = 15
KV = 5
HD = 64
LEN = 212


EPSILON = 1e-05
THETA_BASE = 100000.0
NEG_FILL = -1e30


def rope_tables(position_ids):
    half_width = HD // 2
    freq_steps = jnp.arange(half_width, dtype=jnp.float32) * (2.0 / HD)
    inverse = jnp.exp(-math.log(THETA_BASE) * freq_steps)
    angles = position_ids.astype(jnp.float32)[:, None] * inverse[None, :]
    cosine = jnp.cos(angles)
    sine_part = jnp.sin(angles)
    return (jnp.concatenate([cosine, cosine], -1), jnp.concatenate([sine_part, sine_part], -1))


def rotate(tensor, cosine, sine_part):
    half_width = HD // 2
    turned = jnp.concatenate([-tensor[..., half_width:], tensor[..., :half_width]], -1)
    return tensor * cosine[:, None, :] + turned * sine_part[:, None, :]


def rotate_back(gradient, cosine, sine_part):
    half_width = HD // 2
    scaled = gradient * sine_part[:, None, :]
    return gradient * cosine[:, None, :] + jnp.concatenate(
        [scaled[..., half_width:], -scaled[..., :half_width]], -1
    )


def norm_forward(values, gain_row):
    inv_rms = lax.rsqrt(jnp.mean(values * values, -1, keepdims=True) + EPSILON)
    return ((values * inv_rms * gain_row.astype(jnp.float32)).astype(jnp.bfloat16), inv_rms)


def norm_backward(values, inv_rms, gain_row, grad_normed):
    weighted = grad_normed * gain_row.astype(jnp.float32)
    gain_grad = jnp.sum(grad_normed * values * inv_rms, 0)
    inner_mean = jnp.mean(weighted * values, -1, keepdims=True)
    return (inv_rms * weighted - values * inv_rms**3 * inner_mean, gain_grad)


def silu_parts(gate_pre):
    sigmoid_val = jax.nn.sigmoid(gate_pre)
    return (gate_pre * sigmoid_val, sigmoid_val * (1.0 + gate_pre * (1.0 - sigmoid_val)))


def attention_forward(queries, keys_in, values_in, allowed):
    length = queries.shape[0]
    groups = H // KV
    scale_factor = HD ** (-0.5)
    query_g = queries.reshape(length, KV, groups, HD)
    scores = (
        jnp.einsum("qkgd,skd->kgqs", query_g, keys_in, preferred_element_type=jnp.float32)
        * scale_factor
    )
    scores = jnp.where(allowed, scores, NEG_FILL)
    highest = jnp.max(scores, -1, keepdims=True)
    raw_weights = jnp.exp(scores - highest)
    totals = jnp.sum(raw_weights, -1, keepdims=True)
    log_total = highest + jnp.log(totals)
    attn_probs = (raw_weights / totals).astype(jnp.bfloat16)
    mixed_vals = jnp.einsum(
        "kgqs,skd->qkgd", attn_probs, values_in, preferred_element_type=jnp.float32
    )
    return (mixed_vals.reshape(length, H * HD).astype(jnp.bfloat16), log_total)


def attention_backward(queries, keys_in, values_in, allowed, log_total, attended, grad_attended):
    length = queries.shape[0]
    groups = H // KV
    scale_factor = HD ** (-0.5)
    query_g = queries.reshape(length, KV, groups, HD)
    scores = (
        jnp.einsum("qkgd,skd->kgqs", query_g, keys_in, preferred_element_type=jnp.float32)
        * scale_factor
    )
    scores = jnp.where(allowed, scores, NEG_FILL)
    attn_probs = jnp.exp(scores - log_total)
    probs_b = attn_probs.astype(jnp.bfloat16)
    grad_g = grad_attended.reshape(length, KV, groups, HD)
    attended_g = attended.reshape(length, KV, groups, HD)
    grad_values = jnp.einsum("kgqs,qkgd->skd", probs_b, grad_g, preferred_element_type=jnp.float32)
    grad_probs = jnp.einsum("qkgd,skd->kgqs", grad_g, values_in, preferred_element_type=jnp.float32)
    delta_row = jnp.sum(grad_g.astype(jnp.float32) * attended_g.astype(jnp.float32), -1)
    delta_row = jnp.transpose(delta_row, (1, 2, 0))[..., None]
    grad_scores = (attn_probs * (grad_probs - delta_row) * scale_factor).astype(jnp.bfloat16)
    grad_queries = jnp.einsum(
        "kgqs,skd->qkgd", grad_scores, keys_in, preferred_element_type=jnp.float32
    ).reshape(length, H, HD)
    grad_keys = jnp.einsum(
        "kgqs,qkgd->skd", grad_scores, query_g, preferred_element_type=jnp.float32
    )
    return (grad_queries, grad_keys, grad_values)


ROWS = 224


def others():
    return range(1, lax.axis_size("shard"))


def swap(block, axis, bit):
    size = lax.axis_size(axis)
    return lax.ppermute(block, axis, [(i, i ^ bit) for i in range(size)])


def half_of(block, which, axis=0):
    size = block.shape[axis] // 2
    return lax.dynamic_slice_in_dim(block, which * size, size, axis)


def ordered(first_is_mine, mine, other, axis=0):
    low = jnp.where(first_is_mine, mine, other)
    high = jnp.where(first_is_mine, other, mine)
    return jnp.concatenate([low, high], axis)


def halve_sum(block, axis, bit, axis_dim=0):
    which = (lax.axis_index(axis) // bit) % 2
    sent = half_of(block, 1 - which, axis_dim).astype(jnp.bfloat16)
    kept = half_of(block, which, axis_dim)
    return kept.astype(jnp.float32) + swap(sent, axis, bit).astype(jnp.float32)


def finish_replica(part):
    part = halve_sum(part, "replica", 2)
    size = lax.axis_size("replica")
    bit = 4
    while bit < size:
        sent = part.astype(jnp.bfloat16)
        part = sent.astype(jnp.float32) + swap(sent, "replica", bit).astype(jnp.float32)
        bit *= 2
    part = part.astype(jnp.bfloat16)
    index = lax.axis_index("replica")
    for bit in (2, 1):
        part = ordered((index // bit) % 2 == 0, part, swap(part, "replica", bit))
    return part


def replica_sum(block):
    return finish_replica(halve_sum(block, "replica", 1))


def gather_weights(shard_t, core):
    mine = half_of(shard_t, core)
    got = [swap(mine, "shard", bit) for bit in others()]
    return [shard_t] + [ordered(core == 0, g, swap(g, "replica", 1)) for g in got]


def place(blocks, me):
    rows = blocks[0].shape[0]
    full = jnp.zeros((len(blocks) * rows, blocks[0].shape[1]), blocks[0].dtype)
    for k, block in enumerate(blocks):
        full = lax.dynamic_update_slice(full, block, ((me ^ k) * rows, 0))
    return full


def gather_rows(rows):
    return jnp.concatenate([rows] + [swap(rows, "shard", bit) for bit in others()], 0)


def scatter_rows(partial):
    total = partial[:ROWS]
    for k in others():
        sent = partial[k * ROWS : (k + 1) * ROWS].astype(jnp.bfloat16)
        total = total + swap(sent, "shard", k).astype(jnp.float32)
    return total


def scatter_grad(grad_t, extra, me, core):
    parts = lax.axis_size("shard")
    n = grad_t.shape[0] // parts
    blocks = jnp.concatenate([grad_t.reshape(parts, n, D), extra], 1)
    half = (n + 16) // 2
    sent = lax.dynamic_slice_in_dim(blocks, (1 - core) * half, half, 1).astype(jnp.bfloat16)
    kept = lax.dynamic_slice_in_dim(blocks, core * half, half, 1)
    pair = kept + swap(sent, "replica", 1).astype(jnp.float32)
    total = lax.dynamic_index_in_dim(pair, me, 0, keepdims=False)
    for k in others():
        block = lax.dynamic_index_in_dim(pair, me ^ k, 0, keepdims=False)
        total = total + swap(block.astype(jnp.bfloat16), "shard", k).astype(jnp.float32)
    return total


def dot_f32(left, right, dims):
    return lax.dot_general(left, right, (dims, ((), ())), preferred_element_type=jnp.float32)


def gain_rows(grad):
    parts = lax.axis_size("shard")
    return jnp.pad(grad.reshape(parts, 1, D // parts), ((0, 0), (0, 15), (0, D - D // parts)))


def on_device(
    hidden_in,
    cotangent,
    segment_ids,
    positions,
    w_qkv,
    w_out,
    w_gate,
    w_up,
    w_down,
    gain_attn,
    gain_mlp,
):
    me = lax.axis_index("shard")
    core = lax.axis_index("replica") % 2
    extra_rows = ROWS - LEN
    in_rows = jnp.pad(hidden_in.reshape(LEN, D), ((0, extra_rows), (0, 0)))
    cot_rows = jnp.pad(cotangent.reshape(LEN, D), ((0, extra_rows), (0, 0)))
    flat_rows = in_rows.astype(jnp.float32)
    segment_row = jnp.pad(segment_ids.reshape(LEN), (0, extra_rows), constant_values=-1)
    position_row = jnp.pad(positions.reshape(LEN), (0, extra_rows))
    row_total = ROWS
    row_index = jnp.arange(row_total)
    allowed = (segment_row[:, None] == segment_row[None, :]) & (
        row_index[None, :] <= row_index[:, None]
    )
    cosine, sine_part = rope_tables(position_row)

    gains = jnp.pad(jnp.stack([gain_attn, gain_mlp]), ((0, 6), (0, D - gain_attn.shape[0])))
    qkv_t = w_qkv.T
    payload = jnp.concatenate([half_of(qkv_t, core), gains], 0)
    got = [payload] + [swap(payload, "shard", bit) for bit in others()]
    half = qkv_t.shape[0] // 2
    qkv_blocks = [qkv_t] + [
        ordered(core == 0, g[:half], swap(g[:half], "replica", 1)) for g in got[1:]
    ]
    full_qkv_t = place(qkv_blocks, me)
    gain_full = place([g[half : half + 2, : gain_attn.shape[0]].T for g in got], me)
    gain_a, gain_m = gain_full[:, 0], gain_full[:, 1]
    full_out_t = place(gather_weights(w_out.T, core), me)
    group_cot = gather_rows(cot_rows)

    normed_one, inv_one = norm_forward(flat_rows, gain_a)
    projected = dot_f32(normed_one, full_qkv_t, ((1,), (1,)))
    queries = rotate(projected[:, : H * HD].reshape(row_total, H, HD), cosine, sine_part).astype(
        jnp.bfloat16
    )
    keys_b = rotate(
        projected[:, H * HD : (H + KV) * HD].reshape(row_total, KV, HD), cosine, sine_part
    ).astype(jnp.bfloat16)
    values_b = projected[:, (H + KV) * HD :].reshape(row_total, KV, HD).astype(jnp.bfloat16)
    attended, log_total = attention_forward(queries, keys_b, values_b, allowed)
    middle = flat_rows + dot_f32(attended, full_out_t, ((1,), (1,)))
    normed_two, inv_two = norm_forward(middle, gain_m)
    group_rows = gather_rows(normed_two)
    gate_pre = jnp.dot(group_rows, w_gate, preferred_element_type=jnp.float32)
    up_pre = jnp.dot(group_rows, w_up, preferred_element_type=jnp.float32)
    silu_val, silu_slope = silu_parts(gate_pre)
    activated = (silu_val * up_pre).astype(jnp.bfloat16)
    cot_float = cot_rows.astype(jnp.float32)
    grad_act = dot_f32(group_cot, w_down, ((1,), (1,)))
    grad_up_b = (grad_act * silu_val).astype(jnp.bfloat16)
    grad_gate_b = (grad_act * up_pre * silu_slope).astype(jnp.bfloat16)
    grad_normed = scatter_rows(
        dot_f32(grad_gate_b, w_gate, ((1,), (1,))) + dot_f32(grad_up_b, w_up, ((1,), (1,)))
    )
    sum_gate = replica_sum(dot_f32(group_rows, grad_gate_b, ((0,), (0,))))
    sum_up = replica_sum(dot_f32(group_rows, grad_up_b, ((0,), (0,))))
    sum_down = replica_sum(dot_f32(activated, group_cot, ((0,), (0,))))
    branch_out = scatter_rows(jnp.dot(activated, w_down, preferred_element_type=jnp.float32))
    hidden_out = (middle + branch_out)[:LEN].astype(jnp.bfloat16).reshape(hidden_in.shape)

    back_two, gain_two_grad = norm_backward(middle, inv_two, gain_m, grad_normed)
    grad_middle = cot_float + back_two
    grad_middle_b = grad_middle.astype(jnp.bfloat16)
    sum_out = finish_replica(
        scatter_grad(
            dot_f32(grad_middle_b, attended, ((0,), (0,))), gain_rows(gain_two_grad), me, core
        )
    )
    grad_attended = jnp.dot(
        grad_middle_b, full_out_t, preferred_element_type=jnp.float32
    ).astype(jnp.bfloat16)
    grad_queries, grad_keys, grad_values = attention_backward(
        queries, keys_b, values_b, allowed, log_total, attended, grad_attended
    )
    grad_queries = rotate_back(grad_queries, cosine, sine_part)
    grad_keys = rotate_back(grad_keys, cosine, sine_part)
    grad_proj = jnp.concatenate(
        [
            grad_queries.reshape(row_total, H * HD),
            grad_keys.reshape(row_total, KV * HD),
            grad_values.reshape(row_total, KV * HD),
        ],
        1,
    ).astype(jnp.bfloat16)
    grad_normed_one = jnp.dot(grad_proj, full_qkv_t, preferred_element_type=jnp.float32)
    back_one, gain_one_grad = norm_backward(flat_rows, inv_one, gain_a, grad_normed_one)
    grad_input = (grad_middle + back_one)[:LEN].reshape(hidden_in.shape)
    sum_qkv = finish_replica(
        scatter_grad(
            dot_f32(grad_proj, normed_one, ((0,), (0,))), gain_rows(gain_one_grad), me, core
        )
    )
    n_qkv, n_out = sum_qkv.shape[0] - 16, sum_out.shape[0] - 16
    return (
        hidden_out,
        grad_input,
        sum_qkv[:n_qkv].T.astype(jnp.float32),
        sum_out[:n_out].T.astype(jnp.float32),
        sum_gate.astype(jnp.float32),
        sum_up.astype(jnp.float32),
        sum_down.astype(jnp.float32),
        sum_qkv[n_qkv, : gain_attn.shape[0]].astype(jnp.float32),
        sum_out[n_out, : gain_attn.shape[0]].astype(jnp.float32),
    )


def solution(mesh):
    in_specs = (
        P(("shard", "replica"), None, None),
        P(("shard", "replica"), None, None),
        P(("shard", "replica"), None),
        P(("shard", "replica"), None),
        P(None, "shard"),
        P(None, "shard"),
        P(None, "shard"),
        P(None, "shard"),
        P("shard", None),
        P("shard"),
        P("shard"),
    )
    out_specs = (
        P(("shard", "replica"), None, None),
        P(("shard", "replica"), None, None),
        P(None, "shard"),
        P(None, "shard"),
        P(None, "shard"),
        P(None, "shard"),
        P("shard", None),
        P("shard"),
        P("shard"),
    )
    return jax.shard_map(
        on_device, mesh=mesh, in_specs=in_specs, out_specs=out_specs, check_vma=False
    )
```

```python
import math

import jax
import jax.numpy as jnp
from jax import lax
from jax.sharding import PartitionSpec as P

D = 960
H = 15
KV = 5
HD = 64
LEN = 212


EPSILON = 1e-05
THETA_BASE = 100000.0
NEG_FILL = -1e30


def rope_tables(position_ids):
    half_width = HD // 2
    freq_steps = jnp.arange(half_width, dtype=jnp.float32) * (2.0 / HD)
    inverse = jnp.exp(-math.log(THETA_BASE) * freq_steps)
    angles = position_ids.astype(jnp.float32)[None, :] * inverse[:, None]
    cosine = jnp.cos(angles)
    sine_part = jnp.sin(angles)
    return (jnp.concatenate([cosine, cosine], 0), jnp.concatenate([sine_part, sine_part], 0))


def rotate(tensor, cosine, sine_part):
    half_width = HD // 2
    turned = jnp.concatenate([-tensor[:, half_width:], tensor[:, :half_width]], 1)
    return tensor * cosine + turned * sine_part


def rotate_back(gradient, cosine, sine_part):
    half_width = HD // 2
    scaled = gradient * sine_part
    return gradient * cosine + jnp.concatenate(
        [scaled[:, half_width:], -scaled[:, :half_width]], 1
    )


def norm_forward(values, gain_row):
    inv_rms = lax.rsqrt(jnp.mean(values * values, -1, keepdims=True) + EPSILON)
    return ((values * inv_rms * gain_row.astype(jnp.float32)).astype(jnp.bfloat16), inv_rms)


def norm_backward(values, inv_rms, gain_row, grad_normed):
    weighted = grad_normed * gain_row.astype(jnp.float32)
    gain_grad = jnp.sum(grad_normed * values * inv_rms, 0)
    inner_mean = jnp.mean(weighted * values, -1, keepdims=True)
    return (inv_rms * weighted - values * inv_rms**3 * inner_mean, gain_grad)


def silu_parts(gate_pre):
    sigmoid_val = jax.nn.sigmoid(gate_pre)
    return (gate_pre * sigmoid_val, sigmoid_val * (1.0 + gate_pre * (1.0 - sigmoid_val)))


def masked_scores(queries, keys_in, allowed):
    scores = jnp.einsum("kgdq,kds->kgqs", queries, keys_in, preferred_element_type=jnp.float32)
    return jnp.where(allowed, scores * HD ** (-0.5), NEG_FILL)


def attention_forward(queries, keys_in, values_in, allowed):
    scores = masked_scores(queries, keys_in, allowed)
    highest = jnp.max(scores, -1, keepdims=True)
    raw_weights = jnp.exp(scores - highest)
    totals = jnp.sum(raw_weights, -1, keepdims=True)
    log_total = highest + jnp.log(totals)
    attn_probs = (raw_weights / totals).astype(jnp.bfloat16)
    mixed_vals = jnp.einsum(
        "kds,kgqs->kgdq", values_in, attn_probs, preferred_element_type=jnp.float32
    )
    return (mixed_vals.astype(jnp.bfloat16), log_total)


def attention_backward(queries, keys_in, values_in, allowed, log_total, attended, grad_g):
    scores = masked_scores(queries, keys_in, allowed)
    attn_probs = jnp.exp(scores - log_total)
    probs_b = attn_probs.astype(jnp.bfloat16)
    grad_values = jnp.einsum("kgqs,kgdq->kds", probs_b, grad_g, preferred_element_type=jnp.float32)
    grad_probs = jnp.einsum("kgdq,kds->kgqs", grad_g, values_in, preferred_element_type=jnp.float32)
    delta_row = jnp.sum(grad_g.astype(jnp.float32) * attended.astype(jnp.float32), 2)[..., None]
    grad_scores = (attn_probs * (grad_probs - delta_row) * HD ** (-0.5)).astype(jnp.bfloat16)
    grad_queries = jnp.einsum(
        "kgqs,kds->kgdq", grad_scores, keys_in, preferred_element_type=jnp.float32
    )
    grad_keys = jnp.einsum(
        "kgqs,kgdq->kds", grad_scores, queries, preferred_element_type=jnp.float32
    )
    return (grad_queries, grad_keys, grad_values)


ROWS = 224


def others():
    return range(1, lax.axis_size("shard"))


def swap(block, axis, bit):
    size = lax.axis_size(axis)
    return lax.ppermute(block, axis, [(i, i ^ bit) for i in range(size)])


def half_of(block, which, axis=0):
    size = block.shape[axis] // 2
    return lax.dynamic_slice_in_dim(block, which * size, size, axis)


def ordered(first_is_mine, mine, other, axis=0):
    low = jnp.where(first_is_mine, mine, other)
    high = jnp.where(first_is_mine, other, mine)
    return jnp.concatenate([low, high], axis)


def halve_sum(block, axis, bit, axis_dim=0):
    which = (lax.axis_index(axis) // bit) % 2
    sent = half_of(block, 1 - which, axis_dim).astype(jnp.bfloat16)
    kept = half_of(block, which, axis_dim)
    return kept.astype(jnp.float32) + swap(sent, axis, bit).astype(jnp.float32)


def exchange_rest(part):
    size = lax.axis_size("replica")
    bit = 4
    while bit < size:
        sent = part.astype(jnp.bfloat16)
        part = sent.astype(jnp.float32) + swap(sent, "replica", bit).astype(jnp.float32)
        bit *= 2
    return part


def spread(part):
    part = part.astype(jnp.bfloat16)
    index = lax.axis_index("replica")
    for bit in (2, 1):
        part = ordered((index // bit) % 2 == 0, part, swap(part, "replica", bit))
    return part


def relative_weights(mine, size, own, core):
    got = [swap(mine, "shard", bit) for bit in others()]
    partner = [swap(g[:size], "replica", 1) for g in got]
    return jnp.concatenate([own] + [g[:size] for g in got] + partner, 0), got


def relative_offset(shard, half, size, me, core):
    parts = lax.axis_size("shard")
    k = me ^ shard
    fetched = jnp.where(core == half, 0, parts - 1)
    return jnp.where(k == 0, half * size, (2 + fetched + k - 1) * size)


def to_absolute(rows, size, me, core):
    pieces = []
    for shard in range(lax.axis_size("shard")):
        for half in (0, 1):
            start = relative_offset(shard, half, size, me, core)
            pieces.append(lax.dynamic_slice_in_dim(rows, start, size, 0))
    return jnp.concatenate(pieces, 0)


def to_relative(rows, size, me, core):
    pieces = [lax.dynamic_slice_in_dim(rows, me * 2 * size, 2 * size, 0)]
    for which in (core, 1 - core):
        for k in others():
            start = ((me ^ k) * 2 + which) * size
            pieces.append(lax.dynamic_slice_in_dim(rows, start, size, 0))
    return jnp.concatenate(pieces, 0)


def gather_rows(rows):
    return jnp.concatenate([rows] + [swap(rows, "shard", bit) for bit in others()], 0)


def scatter_rows(partial):
    total = partial[:ROWS]
    for k in others():
        sent = partial[k * ROWS : (k + 1) * ROWS].astype(jnp.bfloat16)
        total = total + swap(sent, "shard", k).astype(jnp.float32)
    return total


def scatter_grad(left, right, dims, gain_grad, me, core):
    parts = lax.axis_size("shard")
    half = left.shape[0] // parts // 2
    split = left.reshape(parts, 2, half, left.shape[1])
    gains = jnp.pad(
        gain_grad.reshape(parts, 1, D // parts), ((0, 0), (0, 7), (0, D - D // parts))
    )

    def share(which):
        rows = lax.dynamic_index_in_dim(split, which, 1, keepdims=False)
        product = dot_f32(rows.reshape(parts * half, left.shape[1]), right, dims)
        return product.reshape(parts, half, D)

    sent = jnp.concatenate(
        [share(1 - core).astype(jnp.bfloat16), gains.astype(jnp.bfloat16)], 1
    )
    arrived = swap(sent, "replica", 1)

    def block(which):
        return jnp.concatenate(
            [
                lax.dynamic_index_in_dim(kept, which, 0, keepdims=False),
                lax.dynamic_index_in_dim(gains, which, 0, keepdims=False),
            ],
            0,
        ) + lax.dynamic_index_in_dim(arrived, which, 0, keepdims=False).astype(jnp.float32)

    kept = share(core)
    moved = [swap(block(me ^ k).astype(jnp.bfloat16), "shard", k) for k in others()]
    total = block(me)
    for piece in moved:
        total = total + piece.astype(jnp.float32)
    return total


def dot_f32(left, right, dims):
    return lax.dot_general(left, right, (dims, ((), ())), preferred_element_type=jnp.float32)


def on_device(
    hidden_in,
    cotangent,
    segment_ids,
    positions,
    w_qkv,
    w_out,
    w_gate,
    w_up,
    w_down,
    gain_attn,
    gain_mlp,
):
    me = lax.axis_index("shard")
    core = lax.axis_index("replica") % 2
    extra_rows = ROWS - LEN
    in_rows = jnp.pad(hidden_in.reshape(LEN, D), ((0, extra_rows), (0, 0)))
    cot_rows = jnp.pad(cotangent.reshape(LEN, D), ((0, extra_rows), (0, 0)))
    flat_rows = in_rows.astype(jnp.float32)
    segment_row = jnp.pad(segment_ids.reshape(LEN), (0, extra_rows), constant_values=-1)
    position_row = jnp.pad(positions.reshape(LEN), (0, extra_rows))
    row_total = ROWS
    row_index = jnp.arange(row_total)
    allowed = (segment_row[:, None] == segment_row[None, :]) & (
        row_index[None, :] <= row_index[:, None]
    )
    cosine, sine_part = rope_tables(position_row)

    own_gains = gain_attn.shape[0]
    gains = jnp.pad(jnp.stack([gain_attn, gain_mlp]), ((0, 6), (0, D - own_gains)))
    qkv_t = w_qkv.T
    n_qkv = qkv_t.shape[0] // 2
    payload = jnp.concatenate([half_of(qkv_t, core), gains], 0)
    all_qkv, got = relative_weights(payload, n_qkv, qkv_t, core)
    gain_parts = jnp.stack([g[n_qkv : n_qkv + 2, :own_gains] for g in [payload] + got])
    gain_a, gain_m = jnp.concatenate(
        [
            lax.dynamic_index_in_dim(gain_parts, me ^ j, 0, keepdims=False)
            for j in range(lax.axis_size("shard"))
        ],
        1,
    )
    out_t = w_out.T
    n_out = out_t.shape[0] // 2
    cot_sent, out_sent, _ = lax.optimization_barrier((cot_rows, half_of(out_t, core), got))
    all_out, _ = relative_weights(out_sent, n_out, out_t, core)
    group_cot = gather_rows(cot_sent)

    normed_one, inv_one = norm_forward(flat_rows, gain_a)
    projected = to_absolute(dot_f32(all_qkv, normed_one, ((1,), (1,))), n_qkv, me, core)
    heads = projected.reshape(H + 2 * KV, HD, row_total)
    queries = rotate(heads[:H], cosine, sine_part).astype(jnp.bfloat16)
    queries = queries.reshape(KV, H // KV, HD, row_total)
    keys_b = rotate(heads[H : H + KV], cosine, sine_part).astype(jnp.bfloat16)
    values_b = heads[H + KV :].astype(jnp.bfloat16)
    attended, log_total = attention_forward(queries, keys_b, values_b, allowed)
    attended_t = attended.reshape(H * HD, row_total)
    mixed_t = to_absolute(dot_f32(all_out, attended_t, ((1,), (0,))), n_out, me, core)
    middle = flat_rows + mixed_t.T
    normed_two, inv_two = norm_forward(middle, gain_m)
    group_rows = gather_rows(normed_two)
    gate_pre = jnp.dot(group_rows, w_gate, preferred_element_type=jnp.float32)
    up_pre = jnp.dot(group_rows, w_up, preferred_element_type=jnp.float32)
    silu_val, silu_slope = silu_parts(gate_pre)
    activated = (silu_val * up_pre).astype(jnp.bfloat16)
    cot_float = cot_rows.astype(jnp.float32)
    grad_act = dot_f32(group_cot, w_down, ((1,), (1,)))
    grad_up_b = (grad_act * silu_val).astype(jnp.bfloat16)
    grad_gate_b = (grad_act * up_pre * silu_slope).astype(jnp.bfloat16)
    grad_normed = scatter_rows(
        dot_f32(grad_gate_b, w_gate, ((1,), (1,))) + dot_f32(grad_up_b, w_up, ((1,), (1,)))
    )
    feed = (
        halve_sum(dot_f32(group_rows, grad_gate_b, ((0,), (0,))), "replica", 1),
        halve_sum(dot_f32(group_rows, grad_up_b, ((0,), (0,))), "replica", 1),
        halve_sum(dot_f32(activated, group_cot, ((0,), (0,))), "replica", 1),
    )
    grad_normed, feed, activated = lax.optimization_barrier((grad_normed, feed, activated))
    feed = tuple(halve_sum(part, "replica", 2) for part in feed)
    branch_out = scatter_rows(jnp.dot(activated, w_down, preferred_element_type=jnp.float32))
    hidden_out = (middle + branch_out)[:LEN].astype(jnp.bfloat16).reshape(hidden_in.shape)

    back_two, gain_two_grad = norm_backward(middle, inv_two, gain_m, grad_normed)
    grad_middle = cot_float + back_two
    grad_middle_t = grad_middle.astype(jnp.bfloat16).T
    grad_attended = dot_f32(all_out, to_relative(grad_middle_t, n_out, me, core), ((0,), (0,)))
    grad_attended = grad_attended.astype(jnp.bfloat16).reshape(attended.shape)
    grad_attended, feed, hidden_out = lax.optimization_barrier((grad_attended, feed, hidden_out))
    feed = tuple(exchange_rest(part) for part in feed)
    own_out = scatter_grad(
        grad_middle_t, attended_t, ((1,), (1,)), gain_two_grad, me, core
    )
    grad_queries, grad_keys, grad_values = attention_backward(
        queries, keys_b, values_b, allowed, log_total, attended, grad_attended
    )
    grad_queries = rotate_back(grad_queries.reshape(H, HD, row_total), cosine, sine_part)
    grad_keys = rotate_back(grad_keys, cosine, sine_part)
    grad_proj_t = jnp.concatenate([grad_queries, grad_keys, grad_values], 0)
    grad_proj_t = grad_proj_t.reshape(2 * n_qkv * lax.axis_size("shard"), row_total)
    grad_proj_t = grad_proj_t.astype(jnp.bfloat16)
    grad_proj_t, feed, own_out = lax.optimization_barrier((grad_proj_t, feed, own_out))
    grad_normed_one = dot_f32(to_relative(grad_proj_t, n_qkv, me, core), all_qkv, ((0,), (0,)))
    back_one, gain_one_grad = norm_backward(flat_rows, inv_one, gain_a, grad_normed_one)
    grad_input = (grad_middle + back_one)[:LEN].reshape(hidden_in.shape)
    own_qkv = scatter_grad(grad_proj_t, normed_one, ((1,), (0,)), gain_one_grad, me, core)
    sum_gate, sum_up, sum_down = (spread(part) for part in feed)
    sum_out = spread(exchange_rest(halve_sum(own_out, "replica", 2)))
    sum_qkv = spread(exchange_rest(halve_sum(own_qkv, "replica", 2)))

    def weight_rows(summed, half):
        rows = jnp.concatenate([summed[:half], summed[half + 8 : 2 * half + 8]], 0)
        return rows.T.astype(jnp.float32)

    return (
        hidden_out,
        grad_input,
        weight_rows(sum_qkv, n_qkv),
        weight_rows(sum_out, n_out),
        sum_gate.astype(jnp.float32),
        sum_up.astype(jnp.float32),
        sum_down.astype(jnp.float32),
        sum_qkv[n_qkv, :own_gains].astype(jnp.float32),
        sum_out[n_out, :own_gains].astype(jnp.float32),
    )


def solution(mesh):
    in_specs = (
        P(("shard", "replica"), None, None),
        P(("shard", "replica"), None, None),
        P(("shard", "replica"), None),
        P(("shard", "replica"), None),
        P(None, "shard"),
        P(None, "shard"),
        P(None, "shard"),
        P(None, "shard"),
        P("shard", None),
        P("shard"),
        P("shard"),
    )
    out_specs = (
        P(("shard", "replica"), None, None),
        P(("shard", "replica"), None, None),
        P(None, "shard"),
        P(None, "shard"),
        P(None, "shard"),
        P(None, "shard"),
        P("shard", None),
        P("shard"),
        P("shard"),
    )
    return jax.shard_map(
        on_device, mesh=mesh, in_specs=in_specs, out_specs=out_specs, check_vma=False
    )
```

```python
import math

import jax
import jax.numpy as jnp
from jax import lax
from jax.sharding import PartitionSpec as P


D = 960
H = 15
KV = 5
HD = 64
LEN = 212


EPSILON = 1e-05
THETA_BASE = 100000.0
NEG_FILL = -1e30


def rope_tables(position_ids):
    half_width = HD // 2
    freq_steps = jnp.arange(half_width, dtype=jnp.float32) * (2.0 / HD)
    inverse = jnp.exp(-math.log(THETA_BASE) * freq_steps)
    angles = position_ids.astype(jnp.float32)[None, :] * inverse[:, None]
    cosine = jnp.cos(angles)
    sine_part = jnp.sin(angles)
    return (jnp.concatenate([cosine, cosine], 0), jnp.concatenate([sine_part, sine_part], 0))


def rotate(tensor, cosine, sine_part):
    half_width = HD // 2
    turned = jnp.concatenate([-tensor[:, half_width:], tensor[:, :half_width]], 1)
    return tensor * cosine + turned * sine_part


def rotate_back(gradient, cosine, sine_part):
    half_width = HD // 2
    scaled = gradient * sine_part
    return gradient * cosine + jnp.concatenate(
        [scaled[:, half_width:], -scaled[:, :half_width]], 1
    )


def norm_forward(values, gain_row):
    inv_rms = lax.rsqrt(jnp.mean(values * values, -1, keepdims=True) + EPSILON)
    return ((values * inv_rms * gain_row.astype(jnp.float32)).astype(jnp.bfloat16), inv_rms)


def norm_backward(values, inv_rms, gain_row, grad_normed):
    weighted = grad_normed * gain_row.astype(jnp.float32)
    gain_grad = jnp.sum(grad_normed * values * inv_rms, 0)
    inner_mean = jnp.mean(weighted * values, -1, keepdims=True)
    return (inv_rms * weighted - values * inv_rms**3 * inner_mean, gain_grad)


def silu_parts(gate_pre):
    sigmoid_val = jax.nn.sigmoid(gate_pre)
    return (gate_pre * sigmoid_val, sigmoid_val * (1.0 + gate_pre * (1.0 - sigmoid_val)))


def masked_scores(queries, keys_in, allowed):
    scores = jnp.einsum("kgdq,kds->kgqs", queries, keys_in, preferred_element_type=jnp.float32)
    return jnp.where(allowed, scores * HD ** (-0.5), NEG_FILL)


def attention_forward(queries, keys_in, values_in, allowed):
    scores = masked_scores(queries, keys_in, allowed)
    highest = jnp.max(scores, -1, keepdims=True)
    raw_weights = jnp.exp(scores - highest)
    totals = jnp.sum(raw_weights, -1, keepdims=True)
    log_total = highest + jnp.log(totals)
    attn_probs = (raw_weights / totals).astype(jnp.bfloat16)
    mixed_vals = jnp.einsum(
        "kds,kgqs->kgdq", values_in, attn_probs, preferred_element_type=jnp.float32
    )
    return (mixed_vals.astype(jnp.bfloat16), log_total)


def attention_backward(queries, keys_in, values_in, allowed, log_total, attended, grad_g):
    scores = masked_scores(queries, keys_in, allowed)
    attn_probs = jnp.exp(scores - log_total)
    probs_b = attn_probs.astype(jnp.bfloat16)
    grad_values = jnp.einsum("kgqs,kgdq->kds", probs_b, grad_g, preferred_element_type=jnp.float32)
    grad_probs = jnp.einsum("kgdq,kds->kgqs", grad_g, values_in, preferred_element_type=jnp.float32)
    delta_row = jnp.sum(grad_g.astype(jnp.float32) * attended.astype(jnp.float32), 2)[..., None]
    grad_scores = (attn_probs * (grad_probs - delta_row) * HD ** (-0.5)).astype(jnp.bfloat16)
    grad_queries = jnp.einsum(
        "kgqs,kds->kgdq", grad_scores, keys_in, preferred_element_type=jnp.float32
    )
    grad_keys = jnp.einsum(
        "kgqs,kgdq->kds", grad_scores, queries, preferred_element_type=jnp.float32
    )
    return (grad_queries, grad_keys, grad_values)


ROWS = 224


def others():
    return range(1, lax.axis_size("shard"))


def swap(block, axis, bit):
    size = lax.axis_size(axis)
    return lax.ppermute(block, axis, [(i, i ^ bit) for i in range(size)])


def half_of(block, which, axis=0):
    size = block.shape[axis] // 2
    return lax.dynamic_slice_in_dim(block, which * size, size, axis)


def ordered(first_is_mine, mine, other, axis=0):
    low = jnp.where(first_is_mine, mine, other)
    high = jnp.where(first_is_mine, other, mine)
    return jnp.concatenate([low, high], axis)


def halve_sum(block, axis, bit):
    which = (lax.axis_index(axis) // bit) % 2
    sent = half_of(block, 1 - which).astype(jnp.bfloat16)
    arrived = swap(sent, axis, bit)
    return half_of(block, which).astype(jnp.float32) + arrived.astype(jnp.float32)


def exchange_rest(part):
    size = lax.axis_size("replica")
    bit = 4
    while bit < size:
        sent = part.astype(jnp.bfloat16)
        part = sent.astype(jnp.float32) + swap(sent, "replica", bit).astype(jnp.float32)
        bit *= 2
    return part


def spread(part):
    part = part.astype(jnp.bfloat16)
    index = lax.axis_index("replica")
    for bit in (2, 1):
        part = ordered((index // bit) % 2 == 0, part, swap(part, "replica", bit))
    return part


def relative_weights(mine, size, own):
    got = [swap(mine, "shard", bit) for bit in others()]
    partner = [swap(g[:size], "replica", 1) for g in got]
    return jnp.concatenate([own] + [g[:size] for g in got] + partner, 0), got


def relative_offset(shard, half, size, me, core):
    parts = lax.axis_size("shard")
    k = me ^ shard
    fetched = jnp.where(core == half, 0, parts - 1)
    return jnp.where(k == 0, half * size, (2 + fetched + k - 1) * size)


def to_absolute(rows, size, me, core):
    pieces = []
    for shard in range(lax.axis_size("shard")):
        for half in (0, 1):
            start = relative_offset(shard, half, size, me, core)
            pieces.append(lax.dynamic_slice_in_dim(rows, start, size, 0))
    return jnp.concatenate(pieces, 0)


def to_relative(rows, size, me, core):
    pieces = [lax.dynamic_slice_in_dim(rows, me * 2 * size, 2 * size, 0)]
    for which in (core, 1 - core):
        for k in others():
            start = ((me ^ k) * 2 + which) * size
            pieces.append(lax.dynamic_slice_in_dim(rows, start, size, 0))
    return jnp.concatenate(pieces, 0)


def gather_rows(rows):
    return jnp.concatenate([rows] + [swap(rows, "shard", bit) for bit in others()], 0)


def scatter_rows(partial):
    total = partial[:ROWS]
    for k in others():
        sent = partial[k * ROWS : (k + 1) * ROWS].astype(jnp.bfloat16)
        total = total + swap(sent, "shard", k).astype(jnp.float32)
    return total


def scatter_grad(left, right, dims, gain_grad, me, core):
    parts = lax.axis_size("shard")
    half = left.shape[0] // parts // 2
    split = left.reshape(parts, 2, half, left.shape[1])
    gains = jnp.pad(
        gain_grad.reshape(parts, 1, D // parts), ((0, 0), (0, 7), (0, D - D // parts))
    )

    def share(which):
        rows = lax.dynamic_index_in_dim(split, which, 1, keepdims=False)
        product = dot_f32(rows.reshape(parts * half, left.shape[1]), right, dims)
        return product.reshape(parts, half, D)

    sent = jnp.concatenate(
        [share(1 - core).astype(jnp.bfloat16), gains.astype(jnp.bfloat16)], 1
    )
    arrived = swap(sent, "replica", 1)

    def block(which):
        return jnp.concatenate(
            [
                lax.dynamic_index_in_dim(kept, which, 0, keepdims=False),
                lax.dynamic_index_in_dim(gains, which, 0, keepdims=False),
            ],
            0,
        ) + lax.dynamic_index_in_dim(arrived, which, 0, keepdims=False).astype(jnp.float32)

    kept = share(core)
    moved = [swap(block(me ^ k).astype(jnp.bfloat16), "shard", k) for k in others()]
    total = block(me)
    for piece in moved:
        total = total + piece.astype(jnp.float32)
    return total


def dot_f32(left, right, dims):
    return lax.dot_general(left, right, (dims, ((), ())), preferred_element_type=jnp.float32)


def on_device(
    hidden_in,
    cotangent,
    segment_ids,
    positions,
    w_qkv,
    w_out,
    w_gate,
    w_up,
    w_down,
    gain_attn,
    gain_mlp,
):
    me = lax.axis_index("shard")
    core = lax.axis_index("replica") % 2
    extra_rows = ROWS - LEN
    in_rows = jnp.pad(hidden_in.reshape(LEN, D), ((0, extra_rows), (0, 0)))
    cot_rows = jnp.pad(cotangent.reshape(LEN, D), ((0, extra_rows), (0, 0)))
    flat_rows = in_rows.astype(jnp.float32)
    segment_row = jnp.pad(segment_ids.reshape(LEN), (0, extra_rows), constant_values=-1)
    position_row = jnp.pad(positions.reshape(LEN), (0, extra_rows))
    row_total = ROWS
    row_index = jnp.arange(row_total)
    allowed = (segment_row[:, None] == segment_row[None, :]) & (
        row_index[None, :] <= row_index[:, None]
    )
    cosine, sine_part = rope_tables(position_row)

    own_gains = gain_attn.shape[0]
    gains = jnp.pad(jnp.stack([gain_attn, gain_mlp]), ((0, 6), (0, D - own_gains)))
    qkv_t = w_qkv.T
    n_qkv = qkv_t.shape[0] // 2
    payload = jnp.concatenate([half_of(qkv_t, core), gains], 0)
    all_qkv, got = relative_weights(payload, n_qkv, qkv_t)
    gain_parts = jnp.stack([g[n_qkv : n_qkv + 2, :own_gains] for g in [payload] + got])
    gain_a, gain_m = jnp.concatenate(
        [
            lax.dynamic_index_in_dim(gain_parts, me ^ j, 0, keepdims=False)
            for j in range(lax.axis_size("shard"))
        ],
        1,
    )
    out_t = w_out.T
    n_out = out_t.shape[0] // 2
    cot_sent, out_sent, _ = lax.optimization_barrier((cot_rows, half_of(out_t, core), got))
    all_out, _ = relative_weights(out_sent, n_out, out_t)
    group_cot = gather_rows(cot_sent)

    normed_one, inv_one = norm_forward(flat_rows, gain_a)
    projected = to_absolute(dot_f32(all_qkv, normed_one, ((1,), (1,))), n_qkv, me, core)
    heads = projected.reshape(H + 2 * KV, HD, row_total)
    queries = rotate(heads[:H], cosine, sine_part).astype(jnp.bfloat16)
    queries = queries.reshape(KV, H // KV, HD, row_total)
    keys_b = rotate(heads[H : H + KV], cosine, sine_part).astype(jnp.bfloat16)
    values_b = heads[H + KV :].astype(jnp.bfloat16)
    attended, log_total = attention_forward(queries, keys_b, values_b, allowed)
    attended_t = attended.reshape(H * HD, row_total)
    mixed_t = to_absolute(dot_f32(all_out, attended_t, ((1,), (0,))), n_out, me, core)
    middle = flat_rows + mixed_t.T
    normed_two, inv_two = norm_forward(middle, gain_m)
    group_rows = gather_rows(normed_two)
    gate_pre = jnp.dot(group_rows, w_gate, preferred_element_type=jnp.float32)
    up_pre = jnp.dot(group_rows, w_up, preferred_element_type=jnp.float32)
    silu_val, silu_slope = silu_parts(gate_pre)
    activated = (silu_val * up_pre).astype(jnp.bfloat16)
    cot_float = cot_rows.astype(jnp.float32)
    grad_act = dot_f32(group_cot, w_down, ((1,), (1,)))
    grad_up_b = (grad_act * silu_val).astype(jnp.bfloat16)
    grad_gate_b = (grad_act * up_pre * silu_slope).astype(jnp.bfloat16)
    grad_parts = dot_f32(grad_gate_b, w_gate, ((1,), (1,))) + dot_f32(
        grad_up_b, w_up, ((1,), (1,))
    )
    grad_normed = scatter_rows(grad_parts)
    feed = (
        halve_sum(dot_f32(group_rows, grad_gate_b, ((0,), (0,))), "replica", 1),
        halve_sum(dot_f32(group_rows, grad_up_b, ((0,), (0,))), "replica", 1),
        halve_sum(dot_f32(activated, group_cot, ((0,), (0,))), "replica", 1),
    )
    feed = tuple(halve_sum(part, "replica", 2) for part in feed)
    grad_normed, activated = lax.optimization_barrier((grad_normed, activated))
    branch_parts = jnp.dot(activated, w_down, preferred_element_type=jnp.float32)
    branch_out = scatter_rows(branch_parts)
    hidden_out = (middle + branch_out)[:LEN].astype(jnp.bfloat16).reshape(hidden_in.shape)

    back_two, gain_two_grad = norm_backward(middle, inv_two, gain_m, grad_normed)
    grad_middle = cot_float + back_two
    grad_middle_t = grad_middle.astype(jnp.bfloat16).T
    grad_attended = dot_f32(all_out, to_relative(grad_middle_t, n_out, me, core), ((0,), (0,)))
    grad_attended = grad_attended.astype(jnp.bfloat16).reshape(attended.shape)
    grad_attended, feed = lax.optimization_barrier((grad_attended, feed))
    feed = tuple(exchange_rest(part) for part in feed)
    own_out = scatter_grad(
        grad_middle_t, attended_t, ((1,), (1,)), gain_two_grad, me, core
    )
    grad_queries, grad_keys, grad_values = attention_backward(
        queries, keys_b, values_b, allowed, log_total, attended, grad_attended
    )
    grad_queries = rotate_back(grad_queries.reshape(H, HD, row_total), cosine, sine_part)
    grad_keys = rotate_back(grad_keys, cosine, sine_part)
    grad_proj_t = jnp.concatenate([grad_queries, grad_keys, grad_values], 0)
    grad_proj_t = grad_proj_t.reshape(2 * n_qkv * lax.axis_size("shard"), row_total)
    grad_proj_t = grad_proj_t.astype(jnp.bfloat16)
    grad_normed_one = dot_f32(to_relative(grad_proj_t, n_qkv, me, core), all_qkv, ((0,), (0,)))
    back_one, gain_one_grad = norm_backward(flat_rows, inv_one, gain_a, grad_normed_one)
    grad_input = (grad_middle + back_one)[:LEN].reshape(hidden_in.shape)
    own_qkv = scatter_grad(grad_proj_t, normed_one, ((1,), (0,)), gain_one_grad, me, core)
    sum_gate, sum_up, sum_down = (spread(part) for part in feed)
    own_both = jnp.concatenate([own_qkv, own_out], 0)
    both = spread(exchange_rest(halve_sum(own_both, "replica", 2)))
    stride = own_both.shape[0]
    out_at = n_qkv + 8

    def weight_rows(start, half):
        rows = [both[start : start + half], both[stride + start : stride + start + half]]
        return jnp.concatenate(rows, 0).T.astype(jnp.float32)

    return (
        hidden_out,
        grad_input,
        weight_rows(0, n_qkv),
        weight_rows(out_at, n_out),
        sum_gate.astype(jnp.float32),
        sum_up.astype(jnp.float32),
        sum_down.astype(jnp.float32),
        both[n_qkv, :own_gains].astype(jnp.float32),
        both[out_at + n_out, :own_gains].astype(jnp.float32),
    )


def solution(mesh):
    in_specs = (
        P(("shard", "replica"), None, None),
        P(("shard", "replica"), None, None),
        P(("shard", "replica"), None),
        P(("shard", "replica"), None),
        P(None, "shard"),
        P(None, "shard"),
        P(None, "shard"),
        P(None, "shard"),
        P("shard", None),
        P("shard"),
        P("shard"),
    )
    out_specs = (
        P(("shard", "replica"), None, None),
        P(("shard", "replica"), None, None),
        P(None, "shard"),
        P(None, "shard"),
        P(None, "shard"),
        P(None, "shard"),
        P("shard", None),
        P("shard"),
        P("shard"),
    )

    return jax.shard_map(
        on_device, mesh=mesh, in_specs=in_specs, out_specs=out_specs, check_vma=False
    )
```
